32 devices in a mesh: groups: 2 (over y), dp: 4 (over z), seq: 4 (over x, core).
Axes of the slice: x: 2, y: 2, z: 4, core: 2. Of those that a mesh axis runs over, the one named last changes fastest.
Arguments:
- query_rows: bfloat16 [8, 1024, 8192], P(('groups', 'dp'), 'seq'), parts along dimension 0, may hold values from -60 to 60
- key_rows: bfloat16 [8, 1024, 1024], P(('groups', 'dp'), 'seq'), parts along dimension 0, may hold values from -4 to 4
- placed_value_rows: bfloat16 [8, 1024, 1024], P(('groups', 'dp'), 'seq'), parts along dimension 0, may hold values from -4 to 4
- doc_lengths: int32 [8, 8], P(('groups', 'dp')), parts along dimension 0, may hold values from 1 to 512, 1024 in all within a row
- span_order: int32 [8, 8], P(('groups', 'dp')), parts along dimension 0, may hold values from 0 to 7, each once within a row
- out_weight: bfloat16 [8192, 8192], P('dp', 'seq'), may hold values from -0.25 to 0.25
Outputs:
- whitened: float32 [32, 512, 8192], P(('groups', 'seq'), None, 'dp'), parts along dimension 0
The draws below stay inside these ranges and needn't reach their ends.
There are 2 independent parts, one for each index of `groups`. The reference program is written for one: setup_inputs(seed, part) draws one part's arguments, and reference() takes and returns one part's arrays. A program takes and returns all parts, laid end to end along the dimension named above; an argument that names none is the same for every part. Nothing has to cross between parts.
All inputs are finite; a program needn't handle non-finite values.
Results may differ from the reference program's by a relative error of at most 0.00073.
Values may be sent and summed in bfloat16 or wider, within the bound.
A program may use at most 128 MiB of HBM per device.

```python
import math
import jax
import jax.numpy as jnp
import numpy as np
from jax import lax

D_OUT = 8192
QUERY_HEADS = 64
KEY_VALUE_HEADS = 8
HEAD_SIZE = 128
BLOCK_W = 512
NDOCS = 8
SPAN = 128
NCHUNK = 8
SEQUENCE_LENGTH = 1024
SEQUENCE_COUNT = 4
NB = 16


def draw_pair(key):
    base = jax.random.fold_in(key, 7)
    first_key, second_key = jax.random.split(base, 2)
    head_group = QUERY_HEADS // KEY_VALUE_HEADS
    key_dimensions = (SEQUENCE_COUNT, SEQUENCE_LENGTH, KEY_VALUE_HEADS, HEAD_SIZE)
    query_dimensions = (SEQUENCE_COUNT, SEQUENCE_LENGTH, KEY_VALUE_HEADS, head_group, HEAD_SIZE)
    key_portion = jnp.clip(jax.random.normal(first_key, key_dimensions, jnp.float32), -4.0, 4.0)
    query_portion = jnp.clip(jax.random.normal(second_key, query_dimensions, jnp.float32), -4.0, 4.0)
    return (query_portion.reshape(SEQUENCE_COUNT, SEQUENCE_LENGTH, QUERY_HEADS * HEAD_SIZE), key_portion.reshape(SEQUENCE_COUNT, SEQUENCE_LENGTH, KEY_VALUE_HEADS * HEAD_SIZE))


def draw_query_rows(key, part):
    query_portion, key_portion = draw_pair(key)
    return query_portion.astype(jnp.bfloat16)


def draw_key_rows(key, part):
    query_portion, key_portion = draw_pair(key)
    return key_portion.astype(jnp.bfloat16)


def steps_of(stream_key, dims, cuts, low, high):
    gain, own = 1.0, jax.random.fold_in(stream_key, 6)
    for position, blocks in cuts:
        draws = jnp.exp(jax.random.uniform(jax.random.fold_in(own, position), (blocks,), jnp.float32, low / len(cuts), high / len(cuts)))
        gain = gain * jnp.repeat(draws, dims[position] // blocks).reshape([-1 if axis == position else 1 for axis in range(len(dims))])
    return gain


def split_up(amount, total, most, skew):
    weights = [(1 << 20) // math.isqrt(grade ** skew) + 1 for grade in range(2, amount + 1)]
    rest, given = total - most - (amount - 1), [1] * (amount - 1)
    while rest > 0:
        candidates = [i for i in range(amount - 1) if given[i] < most]
        mass, budget = sum([weights[i] for i in candidates]), rest
        for i in candidates:
            more = min(most - given[i], max(1, budget * weights[i] // mass), rest)
            given[i] = given[i] + more
            rest = rest - more
    return np.array([most] + given)


def ragged_sizes(own_key, amount, total, most, slope):
    if amount == 2:
        one = jax.random.randint(own_key, (), max(1, total - most), min(most, total - 1) + 1)
        return jnp.stack([one, total - one])
    sizes = jnp.asarray(split_up(amount, total, most, slope), jnp.int32)
    couples = (amount - 1) // 2
    donor, receiver = sizes[1:1 + 2 * couples:2], sizes[2:2 + 2 * couples:2]
    room = jnp.minimum(donor - 1, most - receiver)
    shifted = jax.random.randint(jax.random.fold_in(own_key, 1), (couples,), 0, 1 << 20) % (room + 1)
    sizes = sizes.at[1:1 + 2 * couples:2].set(donor - shifted).at[2:2 + 2 * couples:2].set(receiver + shifted)
    return sizes[jax.random.permutation(jax.random.fold_in(own_key, 2), amount)]


def gaussian(own_key, dims, deviation, bound, shards=(), kind=jnp.bfloat16):
    factor_of = steps_of(own_key, dims, shards, -0.22, 0.18) if shards else 1.0
    drawn = jax.random.normal(own_key, dims, jnp.float32) * deviation * factor_of
    return jnp.minimum(jnp.maximum(drawn, -bound), bound).astype(kind)


def setup_inputs(seed: int = 0, part: int = 0) -> dict:
    splits = jax.random.split(jax.random.key(seed), 7)
    own_keys = jax.random.split(jax.random.fold_in(splits[6], part), 7)
    return {
        "query_rows": draw_query_rows(jax.random.fold_in(jax.random.fold_in(splits[6], part), 71), part),
        "key_rows": draw_key_rows(jax.random.fold_in(jax.random.fold_in(splits[6], part), 71), part),
        "placed_value_rows": gaussian(own_keys[2], (SEQUENCE_COUNT, SEQUENCE_LENGTH, KEY_VALUE_HEADS * HEAD_SIZE), 1.0, 4.0, ((0, 4), (1, 4))),
        "doc_lengths": jax.vmap(lambda own: ragged_sizes(own, NDOCS, SEQUENCE_LENGTH, SEQUENCE_LENGTH // 2, 2))(jax.random.split(own_keys[3], SEQUENCE_COUNT)).reshape((SEQUENCE_COUNT, NDOCS)).astype(jnp.int32),
        "span_order": jax.vmap(lambda own: jax.random.permutation(own, NCHUNK))(jax.random.split(own_keys[4], SEQUENCE_COUNT)).reshape((SEQUENCE_COUNT, NCHUNK)).astype(jnp.int32),
        "out_weight": gaussian(splits[5], (D_OUT, QUERY_HEADS * HEAD_SIZE), BLOCK_W ** -0.5, 0.25, ((0, 4), (1, 4))),
    }


def doc_numbers(positions, lengths):
    starts = jnp.cumsum(lengths) - lengths
    return jnp.sum((positions[:, None] >= starts[None, :]).astype(jnp.int32), axis=1).astype(jnp.int32)

def sequence_grams(query_seq, key_seq, value_seq, length_seq, order_seq):
    row_ids = jnp.arange(SEQUENCE_LENGTH, dtype=jnp.int32)
    positions = (order_seq[row_ids // SPAN] * SPAN + row_ids % SPAN).astype(jnp.int32)
    doc_ids = doc_numbers(positions, length_seq)
    visible = (doc_ids[:, None] == doc_ids[None, :]) & (positions[None, :] <= positions[:, None])
    head_group = QUERY_HEADS // KEY_VALUE_HEADS

    def one_head(head_index):
        query_head = lax.dynamic_slice_in_dim(query_seq, head_index * HEAD_SIZE, HEAD_SIZE, 1)
        key_head = lax.dynamic_slice_in_dim(key_seq, head_index // head_group * HEAD_SIZE, HEAD_SIZE, 1)
        value_head = lax.dynamic_slice_in_dim(value_seq, head_index // head_group * HEAD_SIZE, HEAD_SIZE, 1)
        scores = lax.dot_general(query_head.astype(jnp.float32), key_head.astype(jnp.float32), (((1,), (1,)), ((), ())), preferred_element_type=jnp.float32) * HEAD_SIZE ** (-0.5)
        scores = jnp.where(visible, scores, -1e+30)
        largest = jnp.max(scores, axis=1, keepdims=True)
        lifted = jnp.exp(scores - largest)
        weights = (lifted / jnp.sum(lifted, axis=1, keepdims=True)).astype(jnp.bfloat16)
        return jnp.dot(weights.astype(jnp.float32), value_head.astype(jnp.float32), preferred_element_type=jnp.float32)
    per_head = lax.map(one_head, jnp.arange(QUERY_HEADS, dtype=jnp.int32))
    outputs = jnp.transpose(per_head, (1, 0, 2)).reshape(SEQUENCE_LENGTH, NB, BLOCK_W)
    return jnp.einsum('rbi,rbj->bij', outputs, outputs, precision=lax.Precision.HIGHEST)

def reference(query_rows, key_rows, placed_value_rows, doc_lengths, span_order, out_weight):

    def accumulate(carry, items):
        query_seq, key_seq, value_seq, length_seq, order_seq = items
        return (carry + sequence_grams(query_seq, key_seq, value_seq, length_seq, order_seq), None)
    begin = jnp.zeros((NB, BLOCK_W, BLOCK_W), jnp.float32)
    grams, ignored = lax.scan(accumulate, begin, (query_rows, key_rows, placed_value_rows, doc_lengths, span_order))
    traces = jnp.trace(grams, axis1=1, axis2=2)
    identity = jnp.eye(BLOCK_W, dtype=jnp.float32)
    damped = grams + (0.1 * traces / BLOCK_W)[:, None, None] * identity
    upper = jnp.swapaxes(jnp.linalg.cholesky(damped), 1, 2)
    weight_blocks = out_weight.astype(jnp.float32).reshape(D_OUT, NB, BLOCK_W)
    return jnp.einsum('bij,obj->bio', upper, weight_blocks, precision=lax.Precision.HIGHEST)
```

```python
import functools

import jax
import jax.numpy as jnp
from jax import lax
from jax.experimental import pallas as pl
from jax.experimental.pallas import tpu as pltpu
from jax.sharding import PartitionSpec as P

QUERY_HEADS = 64
KEY_VALUE_HEADS = 8
HEAD_SIZE = 128
BLOCK_W = 512
NB = 16
TILE = 128
TILES = BLOCK_W // TILE
OFFSETS = [sum(TILES - t for t in range(i)) * TILE for i in range(TILES + 1)]
PACKED = OFFSETS[TILES]
F32 = jnp.float32
BF16 = jnp.bfloat16


def widths(count):
    out, step = [], 1
    while len(out) == 0 or out[-1] < count:
        out.append(min(count, (out[-1] if out else 0) + step))
        if len(out) >= 8:
            step = 4
    return out


def attention_kernel(span, spans, blocks, lengths_ref, order_ref, q_ref, k_ref, v_ref, gram_ref,
                     k_pos, v_pos, hi_ref, lo_ref):
    b = pl.program_id(0)
    heads = BLOCK_W // HEAD_SIZE

    @pl.when(b % (QUERY_HEADS // KEY_VALUE_HEADS // heads) == 0)
    def _():
        for r in range(spans):
            at = pl.multiple_of(order_ref[0, r] * span, span)
            k_pos[pl.ds(at, span), :] = k_ref[r * span:(r + 1) * span, :]
            v_pos[pl.ds(at, span), :] = v_ref[r * span:(r + 1) * span, :]

    def one_span(r, carry):
        place = order_ref[0, r]
        base = place * span
        pos = base + lax.broadcasted_iota(jnp.int32, (span, 1), 0)
        start = jnp.zeros((span, 1), jnp.int32)
        first = jnp.int32(0)
        total = jnp.int32(0)
        for d in range(lengths_ref.shape[1]):
            start = jnp.where(pos >= total, total, start)
            first = jnp.where(base >= total, total, first)
            total = total + lengths_ref[0, d]
        low = first // span
        needed = place - low + 1
        row = pl.multiple_of(r * span, span)

        def attend(count):
            begin = jnp.minimum(low, spans - count)
            at = pl.multiple_of(begin * span, span)
            keys = k_pos[pl.ds(at, count * span), :]
            values = v_pos[pl.ds(at, count * span), :]
            key_pos = begin * span + lax.broadcasted_iota(jnp.int32, (span, count * span), 1)
            visible = (key_pos >= start) & (key_pos <= pos)
            for h in range(heads):
                query = q_ref[pl.ds(row, span), h * HEAD_SIZE:(h + 1) * HEAD_SIZE]
                scores = lax.dot_general(query, keys, (((1,), (1,)), ((), ())),
                                         preferred_element_type=F32) * HEAD_SIZE ** (-0.5)
                scores = jnp.where(visible, scores, -1e30)
                lifted = jnp.exp(scores - jnp.max(scores, axis=1, keepdims=True))
                weights = (lifted * (1.0 / jnp.sum(lifted, axis=1, keepdims=True))).astype(BF16)
                mixed = jnp.dot(weights, values, preferred_element_type=F32)
                high = mixed.astype(BF16)
                hi_ref[pl.ds(row, span), h * HEAD_SIZE:(h + 1) * HEAD_SIZE] = high
                lo_ref[pl.ds(row, span), h * HEAD_SIZE:(h + 1) * HEAD_SIZE] = (
                    mixed - high.astype(F32)).astype(BF16)

        below = 0
        for count in widths(spans):
            pl.when((needed > below) & (needed <= count))(functools.partial(attend, count))
            below = count
        return carry

    lax.fori_loop(0, spans, one_span, 0)
    dims = (((0,), (0,)), ((), ()))
    for i in range(TILES):
        hi_l = hi_ref[:, i * TILE:(i + 1) * TILE]
        lo_l = lo_ref[:, i * TILE:(i + 1) * TILE]
        hi_r = hi_ref[:, i * TILE:]
        lo_r = lo_ref[:, i * TILE:]
        gram_ref[0, :, OFFSETS[i]:OFFSETS[i + 1]] = (
            lax.dot_general(hi_l, hi_r, dims, preferred_element_type=F32)
            + lax.dot_general(hi_l, lo_r, dims, preferred_element_type=F32)
            + lax.dot_general(lo_l, hi_r, dims, preferred_element_type=F32))


def attention_grams(query, keys, values, lengths, order, span):
    rows, columns = query.shape
    spans, blocks = rows // span, columns // BLOCK_W
    per_kv = QUERY_HEADS // KEY_VALUE_HEADS * HEAD_SIZE // BLOCK_W
    smem = pl.BlockSpec(memory_space=pltpu.SMEM)
    return pl.pallas_call(
        functools.partial(attention_kernel, span, spans, blocks),
        grid=(blocks,),
        out_shape=jax.ShapeDtypeStruct((blocks, TILE, PACKED), F32),
        in_specs=[
            smem, smem,
            pl.BlockSpec((rows, BLOCK_W), lambda b: (0, b)),
            pl.BlockSpec((rows, HEAD_SIZE), lambda b: (0, b // per_kv)),
            pl.BlockSpec((rows, HEAD_SIZE), lambda b: (0, b // per_kv)),
        ],
        out_specs=pl.BlockSpec((1, TILE, PACKED), lambda b: (b, 0, 0)),
        scratch_shapes=[
            pltpu.VMEM((rows, HEAD_SIZE), BF16),
            pltpu.VMEM((rows, HEAD_SIZE), BF16),
            pltpu.VMEM((rows, BLOCK_W), BF16),
            pltpu.VMEM((rows, BLOCK_W), BF16),
        ],
        name="attention_grams",
    )(lengths, order, query, keys, values)


def split3(x):
    high = x.astype(BF16)
    rest = x - high.astype(F32)
    mid = rest.astype(BF16)
    return high, mid, (rest - mid.astype(F32)).astype(BF16)


def outer6(left, right, axis=0):
    lh, lm, ll = split3(left)
    rh, rm, rl = split3(right)
    lhs = jnp.concatenate([lh, lh, lm, lh, ll, lm], axis=0)
    rhs = jnp.concatenate([rh, rm, rh, rl, rh, rm], axis=0)
    return lax.dot_general(lhs, rhs, (((0,), (0,)), ((), ())), preferred_element_type=F32)


def factor_panel(a_ref, i):
    lo, hi = OFFSETS[i], OFFSETS[i + 1]
    tiles = TILES - i
    sub = lax.broadcasted_iota(jnp.int32, (8, TILE), 0)
    for s in range(TILE // 8):
        rows = slice(8 * s, 8 * s + 8)
        strip = [a_ref[rows, lo + t * TILE:lo + (t + 1) * TILE] for t in range(tiles)]
        cols = [jnp.broadcast_to(strip[0][:, 8 * s + j:8 * s + j + 1], (8, TILE)) for j in range(8)]
        for j in range(8):
            inv = lax.rsqrt(cols[j][j:j + 1, :])
            low = jnp.where(sub > j, cols[j] * inv, 0.0)
            own = sub == j
            for m in range(j + 1, 8):
                cols[m] = cols[m] - low * (cols[m][j:j + 1, :] * inv)
            for t in range(tiles):
                row = strip[t][j:j + 1, :] * inv
                strip[t] = jnp.where(own, row, strip[t] - low * row)
        for t in range(tiles):
            a_ref[rows, lo + t * TILE:lo + (t + 1) * TILE] = strip[t]
        if s < TILE // 8 - 1:
            whole = jnp.concatenate(strip, axis=1)
            update = outer6(strip[0], whole)
            a_ref[8 * s + 8:, lo:hi] = a_ref[8 * s + 8:, lo:hi] - update[8 * s + 8:, :]


def cholesky_kernel(gram_ref, out_ref, a_ref):
    a_ref[...] = gram_ref[0]
    eye = (lax.broadcasted_iota(jnp.int32, (TILE, TILE), 0)
           == lax.broadcasted_iota(jnp.int32, (TILE, TILE), 1))
    trace = jnp.zeros((1, 1), F32)
    for i in range(TILES):
        diag = jnp.where(eye, a_ref[:, OFFSETS[i]:OFFSETS[i] + TILE], 0.0)
        trace = trace + jnp.sum(jnp.sum(diag, axis=1, keepdims=True), axis=0, keepdims=True)
    damp = jnp.where(eye, 0.1 * trace / BLOCK_W, 0.0)
    for i in range(TILES):
        at = slice(OFFSETS[i], OFFSETS[i] + TILE)
        a_ref[:, at] = a_ref[:, at] + damp
    upper = (lax.broadcasted_iota(jnp.int32, (TILE, TILE), 0)
             <= lax.broadcasted_iota(jnp.int32, (TILE, TILE), 1))
    for i in range(TILES):
        factor_panel(a_ref, i)
        at = slice(OFFSETS[i], OFFSETS[i] + TILE)
        for t in range(i + 1, TILES):
            left = a_ref[:, OFFSETS[i] + (t - i) * TILE:OFFSETS[i] + (t - i + 1) * TILE]
            right = a_ref[:, OFFSETS[i] + (t - i) * TILE:OFFSETS[i + 1]]
            a_ref[:, OFFSETS[t]:OFFSETS[t + 1]] = (
                a_ref[:, OFFSETS[t]:OFFSETS[t + 1]] - outer6(left, right))
        a_ref[:, at] = jnp.where(upper, a_ref[:, at], 0.0)
    out_ref[0] = a_ref[...]


def factor(grams):
    spec = pl.BlockSpec((1, TILE, PACKED), lambda b: (b, 0, 0))
    return pl.pallas_call(
        cholesky_kernel,
        grid=(grams.shape[0],),
        out_shape=jax.ShapeDtypeStruct(grams.shape, F32),
        in_specs=[spec],
        out_specs=spec,
        scratch_shapes=[pltpu.VMEM((TILE, PACKED), F32)],
        name="factor",
    )(grams)


def whiten_kernel(u_ref, w_ref, out_ref):
    for i in range(TILES):
        upper = u_ref[0, :, OFFSETS[i]:OFFSETS[i + 1]]
        high = upper.astype(BF16)
        low = (upper - high.astype(F32)).astype(BF16)
        weight = w_ref[:, i * TILE:]
        both = lax.dot_general(jnp.concatenate([high, low], axis=0), weight,
                               (((1,), (1,)), ((), ())), preferred_element_type=F32)
        out_ref[0, i * TILE:(i + 1) * TILE, :] = both[:TILE] + both[TILE:]


def whiten(upper, weight):
    blocks, outs = upper.shape[0], weight.shape[0]
    step = min(outs, 1024)
    return pl.pallas_call(
        whiten_kernel,
        grid=(blocks, outs // step),
        out_shape=jax.ShapeDtypeStruct((blocks, BLOCK_W, outs), F32),
        in_specs=[
            pl.BlockSpec((1, TILE, PACKED), lambda b, o: (b, 0, 0)),
            pl.BlockSpec((step, BLOCK_W), lambda b, o: (o, b)),
        ],
        out_specs=pl.BlockSpec((1, BLOCK_W, step), lambda b, o: (b, 0, o)),
        name="whiten",
    )(upper, weight)


def by_heads(rows, count):
    return lax.all_to_all(rows, "seq", split_axis=1, concat_axis=0, tiled=True)


def shards(query_rows, key_rows, placed_value_rows, doc_lengths, span_order, out_weight):
    tok_count = query_rows.shape[1]
    seq_count = lax.axis_size("seq")
    dp_count = lax.axis_size("dp")
    span = tok_count * seq_count // span_order.shape[1]
    query = by_heads(query_rows[0], seq_count)
    keys = by_heads(key_rows[0], seq_count)
    values = by_heads(placed_value_rows[0], seq_count)
    grams = attention_grams(query, keys, values, doc_lengths, span_order, span)
    if grams.shape[0] % dp_count == 0:
        own = lax.psum_scatter(grams, "dp", scatter_dimension=0, tiled=True)
        upper = lax.all_gather(factor(own), "dp", axis=0, tiled=True)
    else:
        upper = factor(lax.psum(grams, "dp"))
    return whiten(upper, out_weight)


def solution(mesh):
    in_specs = (
        P(("groups", "dp"), "seq", None),
        P(("groups", "dp"), "seq", None),
        P(("groups", "dp"), "seq", None),
        P(("groups", "dp"), None),
        P(("groups", "dp"), None),
        P("dp", "seq"),
    )
    out_specs = P(("groups", "seq"), None, "dp")
    return jax.shard_map(shards, mesh=mesh, in_specs=in_specs, out_specs=out_specs, check_vma=False)
```

```python
import functools

import jax
import jax.numpy as jnp
from jax import lax
from jax.experimental import pallas as pl
from jax.experimental.pallas import tpu as pltpu
from jax.sharding import PartitionSpec as P

QUERY_HEADS = 64
KEY_VALUE_HEADS = 8
HEAD_SIZE = 128
BLOCK_W = 512
NB = 16
TILE = 128
TILES = BLOCK_W // TILE
OFFSETS = [sum(TILES - t for t in range(i)) * TILE for i in range(TILES + 1)]
PACKED = OFFSETS[TILES]
F32 = jnp.float32
BF16 = jnp.bfloat16


def widths(count):
    return [w for w in (1, 2, 3, 4, 5) if w < count] + list(range(8, count, 4)) + [count]


def attention_kernel(span, pieces, lengths_ref, order_ref, me_ref, *refs):
    q_refs, kv_refs = refs[:pieces], refs[pieces:2 * pieces]
    gram_ref, k_pos, v_pos, q_all, hi_ref, lo_ref = refs[2 * pieces:]
    heads = BLOCK_W // HEAD_SIZE
    tok_count = q_refs[0].shape[0]
    local_spans = tok_count // span
    spans = local_spans * pieces
    log2e = 1.4426950408889634

    def first_span(d):
        return lax.rem(me_ref[0] - d + pieces, pieces) * local_spans

    for d in range(pieces):
        q_all[d * tok_count:(d + 1) * tok_count, :] = q_refs[d][...]
        for r in range(local_spans):
            at = pl.multiple_of(order_ref[0, first_span(d) + r] * span, span)
            k_pos[pl.ds(at, span), :] = kv_refs[d][r * span:(r + 1) * span, :HEAD_SIZE]
            v_pos[pl.ds(at, span), :] = kv_refs[d][r * span:(r + 1) * span, HEAD_SIZE:]

    def one_span(t, carry):
        place = order_ref[0, first_span(t // local_spans) + t % local_spans]
        base = place * span
        pos = base + lax.broadcasted_iota(jnp.int32, (span, 1), 0)
        start = jnp.zeros((span, 1), jnp.int32)
        first = jnp.int32(0)
        total = jnp.int32(0)
        for n in range(lengths_ref.shape[1]):
            start = jnp.where(pos >= total, total, start)
            first = jnp.where(base >= total, total, first)
            total = total + lengths_ref[0, n]
        low = first // span
        needed = place - low + 1
        row = pl.multiple_of(t * span, span)

        def attend(count):
            begin = jnp.minimum(low, spans - count)
            at = pl.multiple_of(begin * span, span)
            keys = k_pos[pl.ds(at, count * span), :]
            values = v_pos[pl.ds(at, count * span), :]
            key_pos = begin * span + lax.broadcasted_iota(jnp.int32, (span, count * span), 1)
            bias = jnp.where((key_pos >= start) & (key_pos <= pos), 0.0, -1e30)

            def two_heads(pair, carry):
                columns = [pl.ds(pl.multiple_of((2 * pair + h) * HEAD_SIZE, HEAD_SIZE), HEAD_SIZE) for h in range(2)]
                query = jnp.concatenate([q_all[pl.ds(row, span), c] for c in columns], axis=0)
                scores = lax.dot_general(query, keys, (((1,), (1,)), ((), ())), preferred_element_type=F32)
                scores = (scores.reshape(2, span, count * span) + bias[None]).reshape(2 * span, count * span)
                largest = jnp.max(scores, axis=1, keepdims=True)
                lifted = jnp.exp2((scores - largest) * (HEAD_SIZE ** (-0.5) * log2e))
                weights = (lifted * (1.0 / jnp.sum(lifted, axis=1, keepdims=True))).astype(BF16)
                mixed = jnp.dot(weights, values, preferred_element_type=F32)
                high = mixed.astype(BF16)
                rest = (mixed - high.astype(F32)).astype(BF16)
                for h, c in enumerate(columns):
                    hi_ref[pl.ds(row, span), c] = high[h * span:(h + 1) * span]
                    lo_ref[pl.ds(row, span), c] = rest[h * span:(h + 1) * span]
                return carry

            lax.fori_loop(0, heads // 2, two_heads, 0)

        below = 0
        for count in widths(spans):
            pl.when((needed > below) & (needed <= count))(functools.partial(attend, count))
            below = count
        return carry

    lax.fori_loop(0, spans, one_span, 0)
    dims = (((0,), (0,)), ((), ()))
    for i in range(TILES):
        hi_l = hi_ref[:, i * TILE:(i + 1) * TILE]
        lo_l = lo_ref[:, i * TILE:(i + 1) * TILE]
        hi_r = hi_ref[:, i * TILE:]
        lo_r = lo_ref[:, i * TILE:]
        gram_ref[0, :, OFFSETS[i]:OFFSETS[i + 1]] = (
            lax.dot_general(hi_l, hi_r, dims, preferred_element_type=F32)
            + lax.dot_general(hi_l, lo_r, dims, preferred_element_type=F32)
            + lax.dot_general(lo_l, hi_r, dims, preferred_element_type=F32))


def attention_grams(queries, keys_values, lengths, order, me, span):
    pieces, tok_count = len(queries), queries[0].shape[0]
    rows = pieces * tok_count
    smem = pl.BlockSpec(memory_space=pltpu.SMEM)
    vmem = pl.BlockSpec(memory_space=pltpu.VMEM)
    return pl.pallas_call(
        functools.partial(attention_kernel, span, pieces),
        out_shape=jax.ShapeDtypeStruct((1, TILE, PACKED), F32),
        in_specs=[smem] * 3 + [vmem] * (2 * pieces),
        out_specs=vmem,
        scratch_shapes=[
            pltpu.VMEM((rows, HEAD_SIZE), BF16),
            pltpu.VMEM((rows, HEAD_SIZE), BF16),
            pltpu.VMEM((rows, BLOCK_W), BF16),
            pltpu.VMEM((rows, BLOCK_W), BF16),
            pltpu.VMEM((rows, BLOCK_W), BF16),
        ],
        cost_estimate=pl.CostEstimate(flops=6 * rows * BLOCK_W * BLOCK_W, transcendentals=rows * rows,
                                      bytes_accessed=4 * rows * BLOCK_W),
        compiler_params=pltpu.CompilerParams(vmem_limit_bytes=40 * 2**20),
        name="attention_grams",
    )(lengths, order, me, *queries, *keys_values)


def split3(x):
    high = x.astype(BF16)
    rest = x - high.astype(F32)
    mid = rest.astype(BF16)
    return high, mid, (rest - mid.astype(F32)).astype(BF16)


def outer6(left, right, axis=0):
    lh, lm, ll = split3(left)
    rh, rm, rl = split3(right)
    lhs = jnp.concatenate([lh, lh, lm, lh, ll, lm], axis=0)
    rhs = jnp.concatenate([rh, rm, rh, rl, rh, rm], axis=0)
    return lax.dot_general(lhs, rhs, (((0,), (0,)), ((), ())), preferred_element_type=F32)


def factor_panel(a_ref, i):
    lo, hi = OFFSETS[i], OFFSETS[i + 1]
    tiles = TILES - i
    sub = lax.broadcasted_iota(jnp.int32, (8, TILE), 0)
    for s in range(TILE // 8):
        rows = slice(8 * s, 8 * s + 8)
        strip = [a_ref[rows, lo + t * TILE:lo + (t + 1) * TILE] for t in range(tiles)]
        cols = [jnp.broadcast_to(strip[0][:, 8 * s + j:8 * s + j + 1], (8, TILE)) for j in range(8)]
        for j in range(8):
            inv = lax.rsqrt(cols[j][j:j + 1, :])
            low = jnp.where(sub > j, cols[j] * inv, 0.0)
            own = sub == j
            for m in range(j + 1, 8):
                cols[m] = cols[m] - low * (cols[m][j:j + 1, :] * inv)
            for t in range(tiles):
                row = strip[t][j:j + 1, :] * inv
                strip[t] = jnp.where(own, row, strip[t] - low * row)
        for t in range(tiles):
            a_ref[rows, lo + t * TILE:lo + (t + 1) * TILE] = strip[t]
        if s < TILE // 8 - 1:
            whole = jnp.concatenate(strip, axis=1)
            update = outer6(strip[0], whole)
            a_ref[8 * s + 8:, lo:hi] = a_ref[8 * s + 8:, lo:hi] - update[8 * s + 8:, :]


def cholesky_kernel(gram_ref, out_ref, a_ref):
    a_ref[...] = gram_ref[0]
    eye = (lax.broadcasted_iota(jnp.int32, (TILE, TILE), 0)
           == lax.broadcasted_iota(jnp.int32, (TILE, TILE), 1))
    trace = jnp.zeros((1, 1), F32)
    for i in range(TILES):
        diag = jnp.where(eye, a_ref[:, OFFSETS[i]:OFFSETS[i] + TILE], 0.0)
        trace = trace + jnp.sum(jnp.sum(diag, axis=1, keepdims=True), axis=0, keepdims=True)
    damp = jnp.where(eye, 0.1 * trace / BLOCK_W, 0.0)
    for i in range(TILES):
        at = slice(OFFSETS[i], OFFSETS[i] + TILE)
        a_ref[:, at] = a_ref[:, at] + damp
    upper = (lax.broadcasted_iota(jnp.int32, (TILE, TILE), 0)
             <= lax.broadcasted_iota(jnp.int32, (TILE, TILE), 1))
    for i in range(TILES):
        factor_panel(a_ref, i)
        at = slice(OFFSETS[i], OFFSETS[i] + TILE)
        for t in range(i + 1, TILES):
            left = a_ref[:, OFFSETS[i] + (t - i) * TILE:OFFSETS[i] + (t - i + 1) * TILE]
            right = a_ref[:, OFFSETS[i] + (t - i) * TILE:OFFSETS[i + 1]]
            a_ref[:, OFFSETS[t]:OFFSETS[t + 1]] = (
                a_ref[:, OFFSETS[t]:OFFSETS[t + 1]] - outer6(left, right))
        a_ref[:, at] = jnp.where(upper, a_ref[:, at], 0.0)
    out_ref[0] = a_ref[...]


def factor(grams):
    spec = pl.BlockSpec((1, TILE, PACKED), lambda b: (b, 0, 0))
    return pl.pallas_call(
        cholesky_kernel,
        grid=(grams.shape[0],),
        out_shape=jax.ShapeDtypeStruct(grams.shape, F32),
        in_specs=[spec],
        out_specs=spec,
        scratch_shapes=[pltpu.VMEM((TILE, PACKED), F32)],
        name="factor",
    )(grams)


def whiten_kernel(u_ref, w_ref, out_ref):
    for i in range(TILES):
        upper = u_ref[0, :, OFFSETS[i]:OFFSETS[i + 1]]
        high = upper.astype(BF16)
        low = (upper - high.astype(F32)).astype(BF16)
        weight = w_ref[:, i * TILE:]
        both = lax.dot_general(jnp.concatenate([high, low], axis=0), weight,
                               (((1,), (1,)), ((), ())), preferred_element_type=F32)
        out_ref[0, i * TILE:(i + 1) * TILE, :] = both[:TILE] + both[TILE:]


def whiten(upper, weight):
    blocks, outs = upper.shape[0], weight.shape[0]
    step = min(outs, 1024)
    return pl.pallas_call(
        whiten_kernel,
        grid=(blocks, outs // step),
        out_shape=jax.ShapeDtypeStruct((blocks, BLOCK_W, outs), F32),
        in_specs=[
            pl.BlockSpec((1, TILE, PACKED), lambda b, o: (b, 0, 0)),
            pl.BlockSpec((step, BLOCK_W), lambda b, o: (o, b)),
        ],
        out_specs=pl.BlockSpec((1, BLOCK_W, step), lambda b, o: (b, 0, o)),
        name="whiten",
    )(upper, weight)


def to_owners(rows, width, column, token):
    count, me = lax.axis_size("seq"), lax.axis_index("seq")
    pieces = []
    for d in range(count):
        share = rows.shape[1] // count
        begin = lax.rem(me + d, count) * share + column
        piece = lax.dynamic_slice_in_dim(rows, begin, width, axis=1)
        if d:
            piece, token = lax.optimization_barrier((piece, token))
            piece = lax.ppermute(piece, "seq", [(s, (s + d) % count) for s in range(count)])
        pieces.append(piece)
    return pieces, token


def shards(query_rows, key_rows, placed_value_rows, doc_lengths, span_order, out_weight):
    tok_count = query_rows.shape[1]
    seq_count = lax.axis_size("seq")
    dp_count = lax.axis_size("dp")
    span = tok_count * seq_count // span_order.shape[1]
    me = lax.axis_index("seq").reshape(1).astype(jnp.int32)
    kv_rows = jnp.concatenate(
        [key_rows[0].reshape(tok_count, KEY_VALUE_HEADS, HEAD_SIZE),
         placed_value_rows[0].reshape(tok_count, KEY_VALUE_HEADS, HEAD_SIZE)], axis=2,
    ).reshape(tok_count, 2 * KEY_VALUE_HEADS * HEAD_SIZE)
    per_kv = QUERY_HEADS // KEY_VALUE_HEADS * HEAD_SIZE // BLOCK_W
    token, grams = jnp.zeros((), F32), []
    for b in range(NB // seq_count):
        if b % per_kv == 0:
            width = 2 * HEAD_SIZE
            keys_values, token = to_owners(kv_rows, width, b // per_kv * width, token)
        queries, token = to_owners(query_rows[0], BLOCK_W, b * BLOCK_W, token)
        grams.append(attention_grams(queries, keys_values, doc_lengths, span_order, me, span))
    grams = jnp.concatenate(grams, axis=0)
    if grams.shape[0] % dp_count == 0:
        own = lax.psum_scatter(grams, "dp", scatter_dimension=0, tiled=True)
        upper = lax.all_gather(factor(own), "dp", axis=0, tiled=True)
    else:
        upper = factor(lax.psum(grams, "dp"))
    return whiten(upper, out_weight)


def solution(mesh):
    in_specs = (
        P(("groups", "dp"), "seq", None),
        P(("groups", "dp"), "seq", None),
        P(("groups", "dp"), "seq", None),
        P(("groups", "dp"), None),
        P(("groups", "dp"), None),
        P("dp", "seq"),
    )
    out_specs = P(("groups", "seq"), None, "dp")
    return jax.shard_map(shards, mesh=mesh, in_specs=in_specs, out_specs=out_specs, check_vma=False)
```
